32 devices in a mesh: replica: 8 (over y, x, core), shard: 4 (over z).
Axes of the slice: x: 2, y: 2, z: 4, core: 2. Of those that a mesh axis runs over, the one named last changes fastest.
Arguments:
- inputs: bfloat16 [4096, 2048], P(('replica', 'shard')), may hold values from -6 to 6
- lengths: int32 [8, 8], P('replica'), may hold values from 1 to 256, 512 in all within a row
- ln_gain: float32 [2048], replicated, may hold values from 0.5 to 1.5
- ln_bias: float32 [2048], replicated, may hold values from -3 to 3
- qkv_weight: bfloat16 [2048, 3, 2048], P(None, None, 'shard'), may hold values from -0.125 to 0.125
- qkv_bias: float32 [3, 2048], P(None, 'shard'), may hold values from -3 to 3
- out_weight: bfloat16 [2048, 2048], P('shard'), may hold values from -0.5 to 0.5
- fc1_weight: bfloat16 [2048, 8192], P(None, 'shard'), may hold values from -0.125 to 0.125
- fc1_bias: float32 [8192], P('shard'), may hold values from -3 to 3
- fc2_weight: bfloat16 [8192, 2048], P('shard'), may hold values from -0.0625 to 0.0625
- out_bias: float32 [2048], replicated, may hold values from -3 to 3
- cotangent: bfloat16 [4096, 2048], P(('replica', 'shard')), may hold values from -6 to 6
Outputs:
- output: bfloat16 [4096, 2048], P(('replica', 'shard'))
- input_grad: float32 [4096, 2048], P(('replica', 'shard'))
- ln_gain_grad: float32 [2048], P('shard')
- ln_bias_grad: float32 [2048], P('shard')
- qkv_weight_grad: float32 [2048, 3, 2048], P(None, None, 'shard')
- qkv_bias_grad: float32 [3, 2048], P(None, 'shard')
- out_weight_grad: float32 [2048, 2048], P('shard')
- fc1_weight_grad: float32 [2048, 8192], P(None, 'shard')
- fc1_bias_grad: float32 [8192], P('shard')
- fc2_weight_grad: float32 [8192, 2048], P('shard')
- out_bias_grad: float32 [2048], replicated
The draws below stay inside these ranges and needn't reach their ends.
Inputs may be any that keep to these rules, and one draw needn't show every extreme that they name: Row g of lengths holds the lengths of the 8 sequences of replica group g in order; they add up to 512, and the longest is 256.
All inputs are finite; a program needn't handle non-finite values.
Results may differ from the reference program's by a relative error of at most 0.011.
Values may be sent and summed in bfloat16 or wider, within the bound.
No kernel may reach another device: no remote copies, remote signals or barrier semaphores. Data moves between devices by JAX's collectives and lax.ppermute only.
A program may use at most 320 MiB of HBM per device.

```python
import math
import jax
import jax.numpy as jnp
import numpy as np
from jax import lax

D = 2048
H = 32
HD = 64
ROT = 32
FF = 8192
SEQS_GRP = 8
GRP_TOK = 512
SEQ_MAX = 256
GROUPS = 8
TOKENS = 4096


def steps_of(stream_key, extent, pieces, least, largest):
    gain, own = 1.0, jax.random.fold_in(stream_key, 6)
    for dim, blocks in pieces:
        heights = jnp.exp(jax.random.uniform(jax.random.fold_in(own, dim), (blocks,), jnp.float32, least / len(pieces), largest / len(pieces)))
        gain = gain * jnp.repeat(heights, extent[dim] // blocks).reshape([-1 if axis == dim else 1 for axis in range(len(extent))])
    return gain


def profile(count, total, limit, slope):
    weights = [(1 << 20) // math.isqrt(standing ** slope) + 1 for standing in range(2, count + 1)]
    surplus, holding = total - limit - (count - 1), [1] * (count - 1)
    while surplus > 0:
        free = [i for i in range(count - 1) if holding[i] < limit]
        mass, budget = sum([weights[i] for i in free]), surplus
        for i in free:
            more = min(limit - holding[i], max(1, budget * weights[i] // mass), surplus)
            holding[i] = holding[i] + more
            surplus = surplus - more
    return np.array([limit] + holding)


def uneven_parts(own_key, count, total, reach, slope):
    if count == 2:
        one = jax.random.randint(own_key, (), max(1, total - reach), min(reach, total - 1) + 1)
        return jnp.stack([one, total - one])
    sizes = jnp.asarray(profile(count, total, reach, slope), jnp.int32)
    couples = (count - 1) // 2
    giver, receiver = sizes[1:1 + 2 * couples:2], sizes[2:2 + 2 * couples:2]
    margin = jnp.minimum(giver - 1, reach - receiver)
    shifted = jax.random.randint(jax.random.fold_in(own_key, 1), (couples,), 0, 1 << 20) % (margin + 1)
    sizes = sizes.at[1:1 + 2 * couples:2].set(giver - shifted).at[2:2 + 2 * couples:2].set(receiver + shifted)
    return sizes[jax.random.permutation(jax.random.fold_in(own_key, 2), count)]


def bell_draw(key, shape, deviation, limit, split=(), kind=jnp.bfloat16):
    loudness = steps_of(key, shape, split, -0.22, 0.18) if split else 1.0
    array = jax.random.normal(key, shape, jnp.float32) * deviation * loudness
    return jnp.minimum(jnp.maximum(array, -limit), limit).astype(kind)


def setup_inputs(seed: int = 0) -> dict:
    splits = jax.random.split(jax.random.key(seed), 13)
    inputs = bell_draw(splits[0], (TOKENS, D), 1.0, 6.0, ((0, 32),))
    lengths = jax.vmap(lambda own: uneven_parts(own, SEQS_GRP, GRP_TOK, SEQ_MAX, 2))(jax.random.split(splits[1], GROUPS)).reshape((GROUPS, SEQS_GRP)).astype(jnp.int32)
    ln_gain = jnp.clip(1.0 + 0.1 * jax.random.normal(splits[2], (D,), jnp.float32), 0.5, 1.5)
    ln_bias = bell_draw(splits[3], (D,), 0.3, 3.0, (), jnp.float32)
    qkv_weight = bell_draw(splits[4], (D, 3, D), D ** -0.5, 0.125, ((2, 4),))
    qkv_bias = bell_draw(splits[5], (3, D), 0.3, 3.0, ((1, 4),), jnp.float32)
    out_weight = bell_draw(splits[6], (D, D), (D // 16) ** -0.5, 0.5, ((0, 4),))
    fc1_weight = bell_draw(splits[7], (D, FF), D ** -0.5, 0.125, ((1, 4),))
    fc1_bias = bell_draw(splits[8], (FF,), 0.3, 3.0, ((0, 4),), jnp.float32)
    fc2_weight = bell_draw(splits[9], (FF, D), FF ** -0.5, 0.0625, ((0, 4),))
    out_bias = bell_draw(splits[10], (D,), 0.3, 3.0, (), jnp.float32)
    cotangent = bell_draw(splits[11], (TOKENS, D), 1.0, 6.0, ((0, 32),))
    return {"inputs": inputs, "lengths": lengths, "ln_gain": ln_gain, "ln_bias": ln_bias, "qkv_weight": qkv_weight, "qkv_bias": qkv_bias, "out_weight": out_weight, "fc1_weight": fc1_weight, "fc1_bias": fc1_bias, "fc2_weight": fc2_weight, "out_bias": out_bias, "cotangent": cotangent}


def normalize(x_float):
    mean_row = lax.optimization_barrier(jnp.mean(x_float, axis=-1, keepdims=True))
    centred = x_float - mean_row
    inv_std = lax.rsqrt(lax.optimization_barrier(jnp.mean(centred * centred, axis=-1, keepdims=True)) + 1e-05)
    return (centred * inv_std, inv_std)

def positions(length_row, count):
    ends = jnp.cumsum(length_row, dtype=jnp.int32)
    row_ids = jnp.arange(count, dtype=jnp.int32)
    passed = (row_ids[:, None] >= ends[None, :]).astype(jnp.int32)
    segment = lax.optimization_barrier(jnp.sum(passed, axis=1, dtype=jnp.int32))
    begin = lax.optimization_barrier(jnp.sum(passed * length_row[None, :], axis=1, dtype=jnp.int32))
    offset = (row_ids - begin).astype(jnp.float32)
    freq_ids = jnp.arange(ROT // 2, dtype=jnp.float32)
    inverse = jnp.exp(freq_ids * (-2.0 * math.log(10000.0) / ROT))
    angle_rows = offset[:, None] * inverse[None, :]
    return (segment, row_ids, jnp.cos(angle_rows), jnp.sin(angle_rows))

def rotate(values, cosine, sine):
    half = ROT // 2
    first = values[..., :half]
    second = values[..., half:ROT]
    cos_b = cosine[:, None, :]
    sin_b = sine[:, None, :]
    return jnp.concatenate([first * cos_b - second * sin_b, second * cos_b + first * sin_b, values[..., ROT:]], axis=-1)

def unrotate(values, cosine, sine):
    half = ROT // 2
    first = values[..., :half]
    second = values[..., half:ROT]
    cos_b = cosine[:, None, :]
    sin_b = sine[:, None, :]
    return jnp.concatenate([first * cos_b + second * sin_b, second * cos_b - first * sin_b, values[..., ROT:]], axis=-1)

def gelu_tanh(inner):
    coef = math.sqrt(2.0 / math.pi)
    return 0.5 * inner * (1.0 + jnp.tanh(coef * (inner + 0.044715 * inner * inner * inner)))

def gelu_slope(inner):
    coef = math.sqrt(2.0 / math.pi)
    tangent = jnp.tanh(coef * (inner + 0.044715 * inner * inner * inner))
    return 0.5 * (1.0 + tangent) + 0.5 * inner * (1.0 - tangent * tangent) * coef * (1.0 + 3.0 * 0.044715 * inner * inner)

def allowed_mask(seg_block, row_block, segment, row_ids):
    return (seg_block[:, None] == segment[None, :]) & (row_ids[None, :] <= row_block[:, None])

def attend(query, keys, values, segment, row_ids):
    count, heads = (query.shape[0], query.shape[1])
    block = min(512, count)
    blocks = count // block
    key_float = keys.astype(jnp.float32)
    value_float = values.astype(jnp.float32)

    def per_block(entry):
        q_block, seg_block, row_block = entry
        scores = jnp.einsum('qhd,khd->hqk', q_block.astype(jnp.float32), key_float) * 0.125
        allowed = allowed_mask(seg_block, row_block, segment, row_ids)[None]
        log_total = jnp.log(lax.optimization_barrier(jnp.sum(jnp.where(allowed, jnp.exp(scores), 0.0), axis=-1)))
        probs = jnp.where(allowed, jnp.exp(scores - log_total[..., None]), 0.0).astype(jnp.bfloat16)
        context = jnp.einsum('hqk,khd->qhd', probs.astype(jnp.float32), value_float).astype(jnp.bfloat16)
        return (context, log_total)
    contexts, totals = lax.map(per_block, (query.reshape(blocks, block, heads, HD), segment.reshape(blocks, block), row_ids.reshape(blocks, block)))
    return (contexts.reshape(count, heads, HD), totals)

def attend_back(query, keys, values, totals, grad_context, segment, row_ids):
    count, heads = (query.shape[0], query.shape[1])
    block = min(512, count)
    blocks = count // block
    key_float = keys.astype(jnp.float32)
    value_float = values.astype(jnp.float32)

    def per_block(carry, entry):
        grad_keys, grad_values = carry
        q_block, g_block, total_block, seg_block, row_block = entry
        q_float = q_block.astype(jnp.float32)
        g_float = g_block.astype(jnp.float32)
        scores = jnp.einsum('qhd,khd->hqk', q_float, key_float) * 0.125
        allowed = allowed_mask(seg_block, row_block, segment, row_ids)[None]
        probs = jnp.where(allowed, jnp.exp(scores - total_block[..., None]), 0.0)
        probs_low = probs.astype(jnp.bfloat16).astype(jnp.float32)
        grad_probs = jnp.einsum('qhd,khd->hqk', g_float, value_float)
        grad_scores = (probs * (grad_probs - lax.optimization_barrier(jnp.sum(probs * grad_probs, axis=-1, keepdims=True))) * 0.125).astype(jnp.bfloat16).astype(jnp.float32)
        grad_query = jnp.einsum('hqk,khd->qhd', grad_scores, key_float)
        grad_keys = grad_keys + jnp.einsum('hqk,qhd->khd', grad_scores, q_float)
        grad_values = grad_values + jnp.einsum('hqk,qhd->khd', probs_low, g_float)
        return ((grad_keys, grad_values), grad_query)
    zeros = jnp.zeros(keys.shape, jnp.float32)
    stacked = (query.reshape(blocks, block, heads, HD), grad_context.reshape(blocks, block, heads, HD), totals, segment.reshape(blocks, block), row_ids.reshape(blocks, block))
    (grad_keys, grad_values), grad_queries = lax.scan(per_block, (zeros, zeros), stacked)
    return (grad_queries.reshape(count, heads, HD), grad_keys, grad_values)

def reference(inputs, lengths, ln_gain, ln_bias, qkv_weight, qkv_bias, out_weight, fc1_weight, fc1_bias, fc2_weight, out_bias, cotangent):
    width = inputs.shape[1]
    qkv_flat = qkv_weight.reshape(width, 3 * width)
    group_inputs = inputs.reshape(GROUPS, GRP_TOK, width)
    group_cots = cotangent.reshape(GROUPS, GRP_TOK, width)

    def per_group(carry, entry):
        x_low, length_row, cot_low = entry
        x_float = x_low.astype(jnp.float32)
        x_hat, inv_std = normalize(x_float)
        normed = (x_hat * ln_gain + ln_bias).astype(jnp.bfloat16)
        qkv = (jnp.dot(normed, qkv_flat, preferred_element_type=jnp.float32) + qkv_bias.reshape(-1)).reshape(GRP_TOK, 3, H, HD)
        segment, row_ids, cosine, sine = positions(length_row, GRP_TOK)
        query = rotate(qkv[:, 0], cosine, sine).astype(jnp.bfloat16)
        keys = rotate(qkv[:, 1], cosine, sine).astype(jnp.bfloat16)
        values = qkv[:, 2].astype(jnp.bfloat16)
        context, totals = attend(query, keys, values, segment, row_ids)
        context_flat = context.reshape(GRP_TOK, width)
        pre = jnp.dot(normed, fc1_weight, preferred_element_type=jnp.float32) + fc1_bias
        hidden = gelu_tanh(pre).astype(jnp.bfloat16)
        mixed = jnp.dot(context_flat, out_weight, preferred_element_type=jnp.float32) + jnp.dot(hidden, fc2_weight, preferred_element_type=jnp.float32)
        output = (x_float + mixed + out_bias).astype(jnp.bfloat16)
        grad_out_w = jnp.dot(context_flat.T, cot_low, preferred_element_type=jnp.float32)
        grad_fc2 = jnp.dot(hidden.T, cot_low, preferred_element_type=jnp.float32)
        grad_out_b = lax.optimization_barrier(jnp.sum(cot_low.astype(jnp.float32), axis=0))
        grad_pre = jnp.dot(cot_low, fc2_weight.T, preferred_element_type=jnp.float32) * gelu_slope(pre)
        grad_fc1_b = lax.optimization_barrier(jnp.sum(grad_pre, axis=0))
        grad_pre_low = grad_pre.astype(jnp.bfloat16)
        grad_fc1 = jnp.dot(normed.T, grad_pre_low, preferred_element_type=jnp.float32)
        grad_context = jnp.dot(cot_low, out_weight.T, preferred_element_type=jnp.float32).astype(jnp.bfloat16).reshape(GRP_TOK, H, HD)
        grad_query, grad_keys, grad_values = attend_back(query, keys, values, totals, grad_context, segment, row_ids)
        grad_qkv = jnp.stack([unrotate(grad_query, cosine, sine), unrotate(grad_keys, cosine, sine), grad_values], axis=1).reshape(GRP_TOK, 3 * width)
        grad_qkv_b = lax.optimization_barrier(jnp.sum(grad_qkv, axis=0)).reshape(3, width)
        grad_qkv_low = grad_qkv.astype(jnp.bfloat16)
        grad_qkv_w = jnp.dot(normed.T, grad_qkv_low, preferred_element_type=jnp.float32).reshape(width, 3, width)
        grad_normed = jnp.dot(grad_qkv_low, qkv_flat.T, preferred_element_type=jnp.float32) + jnp.dot(grad_pre_low, fc1_weight.T, preferred_element_type=jnp.float32)
        grad_gain = lax.optimization_barrier(jnp.sum(grad_normed * x_hat, axis=0))
        grad_bias = lax.optimization_barrier(jnp.sum(grad_normed, axis=0))
        scaled = grad_normed * ln_gain
        input_grad = cot_low.astype(jnp.float32) + inv_std * (scaled - lax.optimization_barrier(jnp.mean(scaled, axis=-1, keepdims=True)) - x_hat * lax.optimization_barrier(jnp.mean(scaled * x_hat, axis=-1, keepdims=True)))
        terms = (grad_gain, grad_bias, grad_qkv_w, grad_qkv_b, grad_out_w, grad_fc1, grad_fc1_b, grad_fc2, grad_out_b)
        carry = tuple((total + term for total, term in zip(carry, terms)))
        return (carry, (output, input_grad))
    start = (jnp.zeros((width,), jnp.float32), jnp.zeros((width,), jnp.float32), jnp.zeros((width, 3, width), jnp.float32), jnp.zeros((3, width), jnp.float32), jnp.zeros((width, width), jnp.float32), jnp.zeros(fc1_weight.shape, jnp.float32), jnp.zeros(fc1_bias.shape, jnp.float32), jnp.zeros(fc2_weight.shape, jnp.float32), jnp.zeros((width,), jnp.float32))
    sums, (outputs, input_grads) = lax.scan(per_group, start, (group_inputs, lengths, group_cots))
    grad_gain, grad_bias, grad_qkv_w, grad_qkv_b, grad_out_w, grad_fc1, grad_fc1_b, grad_fc2, grad_out_b = sums
    return (outputs.reshape(TOKENS, width), input_grads.reshape(TOKENS, width), grad_gain, grad_bias, grad_qkv_w, grad_qkv_b, grad_out_w, grad_fc1, grad_fc1_b, grad_fc2, grad_out_b)
```

```python
import math

import jax
import jax.numpy as jnp
from jax import lax
from jax.sharding import PartitionSpec as P

HD = 64
ROT = 32


def normalize(x_float):
    mean_row = jnp.mean(x_float, axis=-1, keepdims=True)
    centred = x_float - mean_row
    inv_std = lax.rsqrt(jnp.mean(centred * centred, axis=-1, keepdims=True) + 1e-05)
    return (centred * inv_std, inv_std)


def positions(length_row, count):
    ends = jnp.cumsum(length_row, dtype=jnp.int32)
    row_ids = jnp.arange(count, dtype=jnp.int32)
    passed = (row_ids[:, None] >= ends[None, :]).astype(jnp.int32)
    segment = jnp.sum(passed, axis=1, dtype=jnp.int32)
    begin = jnp.sum(passed * length_row[None, :], axis=1, dtype=jnp.int32)
    offset = (row_ids - begin).astype(jnp.float32)
    freq_ids = jnp.arange(ROT // 2, dtype=jnp.float32)
    inverse = jnp.exp(freq_ids * (-2.0 * math.log(10000.0) / ROT))
    angle_rows = offset[:, None] * inverse[None, :]
    return (segment, row_ids, jnp.cos(angle_rows), jnp.sin(angle_rows))


def rotate(values, cosine, sine):
    half = ROT // 2
    first = values[..., :half]
    second = values[..., half:ROT]
    cos_b = cosine[:, None, :]
    sin_b = sine[:, None, :]
    return jnp.concatenate(
        [first * cos_b - second * sin_b, second * cos_b + first * sin_b, values[..., ROT:]], axis=-1
    )


def unrotate(values, cosine, sine):
    half = ROT // 2
    first = values[..., :half]
    second = values[..., half:ROT]
    cos_b = cosine[:, None, :]
    sin_b = sine[:, None, :]
    return jnp.concatenate(
        [first * cos_b + second * sin_b, second * cos_b - first * sin_b, values[..., ROT:]], axis=-1
    )


def gelu_tanh(inner):
    coef = math.sqrt(2.0 / math.pi)
    return 0.5 * inner * (1.0 + jnp.tanh(coef * (inner + 0.044715 * inner * inner * inner)))


def gelu_slope(inner):
    coef = math.sqrt(2.0 / math.pi)
    tangent = jnp.tanh(coef * (inner + 0.044715 * inner * inner * inner))
    return 0.5 * (1.0 + tangent) + 0.5 * inner * (1.0 - tangent * tangent) * coef * (
        1.0 + 3.0 * 0.044715 * inner * inner
    )


def allowed_mask(seg_block, row_block, segment, row_ids):
    return (seg_block[:, None] == segment[None, :]) & (row_ids[None, :] <= row_block[:, None])


def attend(query, keys, values, segment, row_ids):
    count, heads = (query.shape[0], query.shape[1])
    block = min(512, count)
    blocks = count // block

    def per_block(entry):
        q_block, seg_block, row_block = entry
        scores = (
            jnp.einsum("qhd,khd->hqk", q_block, keys, preferred_element_type=jnp.float32) * 0.125
        )
        allowed = allowed_mask(seg_block, row_block, segment, row_ids)[None]
        log_total = jnp.log(jnp.sum(jnp.where(allowed, jnp.exp(scores), 0.0), axis=-1))
        probs = jnp.where(allowed, jnp.exp(scores - log_total[..., None]), 0.0).astype(jnp.bfloat16)
        context = jnp.einsum(
            "hqk,khd->qhd", probs, values, preferred_element_type=jnp.float32
        ).astype(jnp.bfloat16)
        return (context, log_total)

    contexts, totals = lax.map(
        per_block,
        (
            query.reshape(blocks, block, heads, HD),
            segment.reshape(blocks, block),
            row_ids.reshape(blocks, block),
        ),
    )
    return (contexts.reshape(count, heads, HD), totals)


def attend_back(query, keys, values, totals, grad_context, segment, row_ids):
    count, heads = (query.shape[0], query.shape[1])
    block = min(512, count)
    blocks = count // block

    def per_block(carry, entry):
        grad_keys, grad_values = carry
        q_block, g_block, total_block, seg_block, row_block = entry
        scores = (
            jnp.einsum("qhd,khd->hqk", q_block, keys, preferred_element_type=jnp.float32) * 0.125
        )
        allowed = allowed_mask(seg_block, row_block, segment, row_ids)[None]
        probs = jnp.where(allowed, jnp.exp(scores - total_block[..., None]), 0.0)
        probs_low = probs.astype(jnp.bfloat16)
        grad_probs = jnp.einsum("qhd,khd->hqk", g_block, values, preferred_element_type=jnp.float32)
        grad_scores = (
            probs * (grad_probs - jnp.sum(probs * grad_probs, axis=-1, keepdims=True)) * 0.125
        ).astype(jnp.bfloat16)
        grad_query = jnp.einsum(
            "hqk,khd->qhd", grad_scores, keys, preferred_element_type=jnp.float32
        )
        grad_keys = grad_keys + jnp.einsum(
            "hqk,qhd->khd", grad_scores, q_block, preferred_element_type=jnp.float32
        )
        grad_values = grad_values + jnp.einsum(
            "hqk,qhd->khd", probs_low, g_block, preferred_element_type=jnp.float32
        )
        return ((grad_keys, grad_values), grad_query)

    zeros = jnp.zeros(keys.shape, jnp.float32)
    stacked = (
        query.reshape(blocks, block, heads, HD),
        grad_context.reshape(blocks, block, heads, HD),
        totals,
        segment.reshape(blocks, block),
        row_ids.reshape(blocks, block),
    )
    (grad_keys, grad_values), grad_queries = lax.scan(per_block, (zeros, zeros), stacked)
    return (grad_queries.reshape(count, heads, HD), grad_keys, grad_values)


def shards(
    inputs,
    lengths,
    ln_gain,
    ln_bias,
    qkv_weight,
    qkv_bias,
    out_weight,
    fc1_weight,
    fc1_bias,
    fc2_weight,
    out_bias,
    cotangent,
):
    rows_dev, width = inputs.shape
    qkv_flat = qkv_weight.reshape(width, -1)
    qkv_cols = qkv_flat.shape[1]
    heads_local = qkv_cols // (3 * HD)
    x_float = inputs.astype(jnp.float32)
    x_hat, inv_std = normalize(x_float)
    normed = (x_hat * ln_gain + ln_bias).astype(jnp.bfloat16)
    normed_full = lax.all_gather(normed, "shard", axis=0, tiled=True)
    qkv_pre = jnp.dot(normed_full, qkv_flat, preferred_element_type=jnp.float32)
    pre = jnp.dot(normed_full, fc1_weight, preferred_element_type=jnp.float32)
    group_rows = qkv_pre.shape[0]
    qkv = (qkv_pre + qkv_bias.reshape(-1)).reshape(group_rows, 3, heads_local, HD)
    segment, row_ids, cosine, sine = positions(lengths[0], group_rows)
    query = rotate(qkv[:, 0], cosine, sine).astype(jnp.bfloat16)
    keys = rotate(qkv[:, 1], cosine, sine).astype(jnp.bfloat16)
    values = qkv[:, 2].astype(jnp.bfloat16)
    context, totals = attend(query, keys, values, segment, row_ids)
    context_flat = context.reshape(group_rows, -1)
    pre = pre + fc1_bias
    hidden = gelu_tanh(pre).astype(jnp.bfloat16)
    mixed = lax.psum_scatter(
        jnp.dot(context_flat, out_weight, preferred_element_type=jnp.float32)
        + jnp.dot(hidden, fc2_weight, preferred_element_type=jnp.float32),
        "shard",
        scatter_dimension=0,
        tiled=True,
    )
    output = (x_float + mixed + out_bias).astype(jnp.bfloat16)
    cot_full = lax.all_gather(cotangent, "shard", axis=0, tiled=True)
    grad_out_w = jnp.dot(context_flat.T, cot_full, preferred_element_type=jnp.float32)
    grad_fc2 = jnp.dot(hidden.T, cot_full, preferred_element_type=jnp.float32)
    grad_out_b = jnp.sum(cot_full, axis=0, dtype=jnp.float32)
    grad_pre = jnp.dot(cot_full, fc2_weight.T, preferred_element_type=jnp.float32) * gelu_slope(pre)
    grad_fc1_b = jnp.sum(grad_pre, axis=0)
    grad_pre_low = grad_pre.astype(jnp.bfloat16)
    grad_fc1 = jnp.dot(normed_full.T, grad_pre_low, preferred_element_type=jnp.float32)
    grad_context = (
        jnp.dot(cot_full, out_weight.T, preferred_element_type=jnp.float32)
        .astype(jnp.bfloat16)
        .reshape(group_rows, heads_local, HD)
    )
    grad_query, grad_keys, grad_values = attend_back(
        query, keys, values, totals, grad_context, segment, row_ids
    )
    grad_qkv = jnp.stack(
        [unrotate(grad_query, cosine, sine), unrotate(grad_keys, cosine, sine), grad_values], axis=1
    ).reshape(group_rows, qkv_cols)
    grad_qkv_b = jnp.sum(grad_qkv, axis=0).reshape(qkv_bias.shape)
    grad_qkv_low = grad_qkv.astype(jnp.bfloat16)
    grad_qkv_w = jnp.dot(normed_full.T, grad_qkv_low, preferred_element_type=jnp.float32).reshape(
        qkv_weight.shape
    )
    grad_normed = lax.psum_scatter(
        jnp.dot(grad_qkv_low, qkv_flat.T, preferred_element_type=jnp.float32)
        + jnp.dot(grad_pre_low, fc1_weight.T, preferred_element_type=jnp.float32),
        "shard",
        scatter_dimension=0,
        tiled=True,
    )
    norm_parts = jnp.stack(
        [jnp.sum(grad_normed * x_hat, axis=0), jnp.sum(grad_normed, axis=0)], axis=0
    )
    norm_shares = lax.psum_scatter(norm_parts, "shard", scatter_dimension=1, tiled=True)
    scaled = grad_normed * ln_gain
    input_grad = cotangent.astype(jnp.float32) + inv_std * (
        scaled
        - jnp.mean(scaled, axis=-1, keepdims=True)
        - x_hat * jnp.mean(scaled * x_hat, axis=-1, keepdims=True)
    )
    grad_qkv_b, grad_fc1_b, grad_out_b, norm_shares = lax.psum(
        (grad_qkv_b, grad_fc1_b, grad_out_b, norm_shares), "replica"
    )
    low_sums = lax.psum(
        tuple(g.astype(jnp.bfloat16) for g in (grad_qkv_w, grad_out_w, grad_fc1, grad_fc2)),
        "replica",
    )
    grad_qkv_w, grad_out_w, grad_fc1, grad_fc2 = (g.astype(jnp.float32) for g in low_sums)
    return (
        output,
        input_grad,
        norm_shares[0],
        norm_shares[1],
        grad_qkv_w,
        grad_qkv_b,
        grad_out_w,
        grad_fc1,
        grad_fc1_b,
        grad_fc2,
        grad_out_b,
    )


def solution(mesh):
    placed = (
        P(("replica", "shard"), None),
        P("replica", None),
        P(),
        P(),
        P(None, None, "shard"),
        P(None, "shard"),
        P("shard", None),
        P(None, "shard"),
        P("shard"),
        P("shard", None),
        P(),
        P(("replica", "shard"), None),
    )
    return jax.shard_map(
        shards,
        mesh=mesh,
        in_specs=placed,
        out_specs=(
            P(("replica", "shard"), None),
            P(("replica", "shard"), None),
            P("shard"),
            P("shard"),
            P(None, None, "shard"),
            P(None, "shard"),
            P("shard", None),
            P(None, "shard"),
            P("shard"),
            P("shard", None),
            P(),
        ),
        check_vma=False,
    )
```

```python
import functools
import math

import jax
import jax.numpy as jnp
from jax import lax
from jax.experimental import pallas as pl
from jax.experimental.pallas import tpu as pltpu
from jax.sharding import PartitionSpec as P

HD = 64
ROT = 32
LANES = 128
BF16 = jnp.bfloat16
F32 = jnp.float32
GELU_C = math.sqrt(2.0 / math.pi)
NT = (((1,), (1,)), ((), ()))
TN = (((0,), (0,)), ((), ()))


def cost(flops, nbytes, trans=0):
    return pl.CostEstimate(flops=int(flops), bytes_accessed=int(nbytes), transcendentals=int(trans))


def tables(length_row, count):
    ends = jnp.cumsum(length_row, dtype=jnp.int32)
    row_ids = jnp.arange(count, dtype=jnp.int32)
    passed = (row_ids[:, None] >= ends[None, :]).astype(jnp.int32)
    segment = jnp.sum(passed, axis=1, dtype=jnp.int32)
    begin = jnp.sum(passed * length_row[None, :], axis=1, dtype=jnp.int32)
    offset = (row_ids - begin).astype(F32)
    lane = jnp.arange(LANES, dtype=jnp.int32) % HD
    half = ROT // 2
    freq = jnp.exp((lane % half).astype(F32) * (-2.0 * math.log(10000.0) / ROT))
    angle = offset[:, None] * freq[None, :]
    cosine, sine = jnp.cos(angle), jnp.sin(angle)
    rot = (lane < ROT)[None, :]
    low = (lane < half)[None, :]
    mul = jnp.where(rot, cosine, 1.0)
    from_up = jnp.where(low, -sine, 0.0)
    from_down = jnp.where(rot & ~low, sine, 0.0)
    allowed = (segment[:, None] == segment[None, :]) & (row_ids[:, None] <= row_ids[None, :])
    bias = jnp.where(allowed, 0.0, -1e30).astype(F32)
    return jnp.stack([mul, from_up, from_down]), bias


def turn(x, tab, sign):
    half = ROT // 2
    up = pltpu.roll(x, LANES - half, 1)
    down = pltpu.roll(x, half, 1)
    return x * tab[0] + sign * (up * tab[1] + down * tab[2])


def norm_kernel(x_ref, gain_ref, bias_ref, o_ref):
    x = x_ref[...].astype(F32)
    mean = jnp.mean(x, axis=-1, keepdims=True)
    cen = x - mean
    inv = lax.rsqrt(jnp.mean(cen * cen, axis=-1, keepdims=True) + 1e-05)
    o_ref[...] = (cen * inv * gain_ref[...] + bias_ref[...]).astype(BF16)


def norm(x, gain, bias):
    return pl.pallas_call(
        norm_kernel, out_shape=jax.ShapeDtypeStruct(x.shape, BF16), name="norm",
        cost_estimate=cost(10 * x.size, 4 * x.size),
    )(x, gain[None], bias[None])


def fc1_kernel(x, w, b, h, s):
    z = jnp.dot(x[...], w[...], preferred_element_type=F32) + b[...]
    z2 = z * z
    t = jnp.tanh(GELU_C * (z + 0.044715 * z * z2))
    h[...] = (0.5 * z * (1.0 + t)).astype(BF16)
    s[...] = (
        0.5 * (1.0 + t) + 0.5 * z * (1.0 - t * t) * GELU_C * (1.0 + 3.0 * 0.044715 * z2)
    ).astype(BF16)


def fc1(x, w, b, tn=512):
    t, d = x.shape
    n = w.shape[1]
    return pl.pallas_call(
        fc1_kernel, out_shape=[jax.ShapeDtypeStruct((t, n), BF16)] * 2, grid=(n // tn,), name="fc1",
        in_specs=[
            pl.BlockSpec((t, d), lambda i: (0, 0)),
            pl.BlockSpec((d, tn), lambda i: (0, i)),
            pl.BlockSpec((1, tn), lambda i: (0, i)),
        ],
        out_specs=[pl.BlockSpec((t, tn), lambda i: (0, i))] * 2,
        cost_estimate=cost(2 * t * d * n, 2 * (t * d + d * n + 2 * t * n)),
    )(x, w, b[None])


def gradpre_kernel(c, w, s, o, bs):
    g = lax.dot_general(c[...], w[...], NT, preferred_element_type=F32) * s[...].astype(F32)
    o[...] = g.astype(BF16)
    bs[...] = jnp.sum(g, axis=0, keepdims=True)


def gradpre(c, w, s, tn=512):
    t, d = c.shape
    n = w.shape[0]
    return pl.pallas_call(
        gradpre_kernel, grid=(n // tn,), name="gradpre",
        out_shape=[jax.ShapeDtypeStruct((t, n), BF16), jax.ShapeDtypeStruct((1, n), F32)],
        in_specs=[
            pl.BlockSpec((t, d), lambda i: (0, 0)),
            pl.BlockSpec((tn, d), lambda i: (i, 0)),
            pl.BlockSpec((t, tn), lambda i: (0, i)),
        ],
        out_specs=[pl.BlockSpec((t, tn), lambda i: (0, i)), pl.BlockSpec((1, tn), lambda i: (0, i))],
        cost_estimate=cost(2 * t * d * n, 2 * (t * d + d * n + 2 * t * n)),
    )(c, w, s)


def qkv_kernel(x, w, b, tab, o):
    part = pl.program_id(0)
    z = jnp.dot(x[...], w[0], preferred_element_type=F32) + b[0]
    cols = z.shape[1]

    @pl.when(part < 2)
    def _():
        for k in range(cols // LANES):
            sl = slice(k * LANES, (k + 1) * LANES)
            o[0, :, sl] = turn(z[:, sl], tab, 1.0).astype(BF16)

    @pl.when(part == 2)
    def _():
        o[0] = z.astype(BF16)


def project(x, w3, b3, tab):
    t, d = x.shape
    n = w3.shape[2]
    return pl.pallas_call(
        qkv_kernel, grid=(3,), name="qkv", out_shape=jax.ShapeDtypeStruct((3, t, n), BF16),
        in_specs=[
            pl.BlockSpec((t, d), lambda i: (0, 0)),
            pl.BlockSpec((1, d, n), lambda i: (i, 0, 0)),
            pl.BlockSpec((1, 1, n), lambda i: (i, 0, 0)),
            pl.BlockSpec((3, t, LANES), lambda i: (0, 0, 0)),
        ],
        out_specs=pl.BlockSpec((1, t, n), lambda i: (i, 0, 0)),
        cost_estimate=cost(6 * t * d * n, 2 * (t * d + 3 * d * n + 3 * t * n)),
    )(x, w3, b3[:, None, :], tab)


def attention_kernel(tile, qkv, gc, tab, bias, ctx, gout, gbias, dk, dv):
    count = gc.shape[0]
    lane = lax.broadcasted_iota(jnp.int32, (1, LANES), 1)
    dk[...] = jnp.zeros_like(dk)
    dv[...] = jnp.zeros_like(dv)
    total_q = jnp.zeros((1, LANES), F32)
    zero = jnp.zeros((), BF16)
    for i in range(count // tile):
        rows = slice(i * tile, (i + 1) * tile)
        keys = slice(0, (i + 1) * tile)
        ctx_i = jnp.zeros((tile, LANES), F32)
        dq_i = jnp.zeros((tile, LANES), F32)
        for h in range(LANES // HD):
            own = (lane >= h * HD) & (lane < (h + 1) * HD)
            qm = jnp.where(own, qkv[0, rows, :], zero)
            gm = jnp.where(own, gc[rows, :], zero)
            km = jnp.where(own, qkv[1, keys, :], zero)
            vm = jnp.where(own, qkv[2, keys, :], zero)
            score = lax.dot_general(qkv[1, keys, :], qm, NT, preferred_element_type=F32)
            e = jnp.exp(score * 0.125 + bias[keys, rows])
            p = e * (1.0 / jnp.sum(e, axis=0, keepdims=True))
            low = p.astype(BF16)
            gp = lax.dot_general(qkv[2, keys, :], gm, NT, preferred_element_type=F32)
            delta = jnp.sum(p * gp, axis=0, keepdims=True)
            ds = (p * (gp - delta) * 0.125).astype(BF16)
            ctx_i += lax.dot_general(low, vm, TN, preferred_element_type=F32)
            dq_i += lax.dot_general(ds, km, TN, preferred_element_type=F32)
            dk[keys, :] += jnp.dot(ds, qm, preferred_element_type=F32)
            dv[keys, :] += jnp.dot(low, gm, preferred_element_type=F32)
        ctx[rows, :] = ctx_i.astype(BF16)
        gq = turn(dq_i, [tab[k, rows, :] for k in range(3)], -1.0)
        gout[0, rows, :] = gq.astype(BF16)
        total_q += jnp.sum(gq, axis=0, keepdims=True)
    gk = turn(dk[...], [tab[k] for k in range(3)], -1.0)
    gout[1] = gk.astype(BF16)
    gout[2] = dv[...].astype(BF16)
    gbias[0] = total_q
    gbias[1] = jnp.sum(gk, axis=0, keepdims=True)
    gbias[2] = jnp.sum(dv[...], axis=0, keepdims=True)


def attention(qkv, gc, tab, bias):
    _, t, n = qkv.shape
    tile = min(256, t)
    return pl.pallas_call(
        functools.partial(attention_kernel, tile), grid=(n // LANES,), name="attention",
        out_shape=[
            jax.ShapeDtypeStruct((t, n), BF16),
            jax.ShapeDtypeStruct((3, t, n), BF16),
            jax.ShapeDtypeStruct((3, 1, n), F32),
        ],
        in_specs=[
            pl.BlockSpec((3, t, LANES), lambda i: (0, 0, i)),
            pl.BlockSpec((t, LANES), lambda i: (0, i)),
            pl.BlockSpec((3, t, LANES), lambda i: (0, 0, 0)),
            pl.BlockSpec((t, t), lambda i: (0, 0)),
        ],
        out_specs=[
            pl.BlockSpec((t, LANES), lambda i: (0, i)),
            pl.BlockSpec((3, t, LANES), lambda i: (0, 0, i)),
            pl.BlockSpec((3, 1, LANES), lambda i: (0, 0, i)),
        ],
        scratch_shapes=[pltpu.VMEM((t, LANES), F32)] * 2,
        cost_estimate=cost(30 * t * t * n, 2 * 8 * t * n, t * t * n // HD),
    )(qkv, gc, tab, bias)


def grad_kernel(idx, ao, ap, bo, bp, send, keep):
    acc = lax.dot_general(ao[...], bo[...], TN, preferred_element_type=F32)
    acc += lax.dot_general(ap[...], bp[...], TN, preferred_element_type=F32)
    low = acc.astype(BF16)
    half = pl.num_programs(0) // 2

    @pl.when(pl.program_id(0) < half)
    def _():
        send[0] = low

    @pl.when(pl.program_id(0) >= half)
    def _():
        keep[0] = low


def grad_rows(plan, ao, ap, bo, bp, at, width):
    t, pieces = ao.shape[0], plan.pieces
    m = ao.shape[1] // (2 * pieces)
    col = at // width
    half = pieces // 2
    shape = jax.ShapeDtypeStruct((half, m, width), BF16)
    return pl.pallas_call(
        grad_kernel, out_shape=[shape, shape], name="grad_rows",
        grid_spec=pltpu.PrefetchScalarGridSpec(
            num_scalar_prefetch=1, grid=(pieces,),
            in_specs=[
                pl.BlockSpec((t, m), lambda j, s: (0, s[0, j])),
                pl.BlockSpec((t, m), lambda j, s: (0, s[1, j])),
                pl.BlockSpec((t, width), lambda j, s: (0, col)),
                pl.BlockSpec((t, width), lambda j, s: (0, col)),
            ],
            out_specs=[
                pl.BlockSpec((1, m, width), lambda j, s: (jnp.minimum(j, half - 1), 0, 0)),
                pl.BlockSpec((1, m, width), lambda j, s: (jnp.maximum(j - half, 0), 0, 0)),
            ],
        ),
        cost_estimate=cost(4 * t * m * pieces * width, 2 * (2 * t * m * pieces + 2 * t * width + m * pieces * width)),
    )(plan.grad_idx, ao, ap, bo, bp)


def grad_cols(plan, ao, ap, bo, bp):
    t, pieces = ao.shape[0], plan.pieces
    m = ao.shape[1]
    width = bo.shape[1] // (2 * pieces)
    half = pieces // 2
    shape = jax.ShapeDtypeStruct((half, m, width), BF16)
    return pl.pallas_call(
        grad_kernel, out_shape=[shape, shape], name="grad_cols",
        grid_spec=pltpu.PrefetchScalarGridSpec(
            num_scalar_prefetch=1, grid=(pieces,),
            in_specs=[
                pl.BlockSpec((t, m), lambda j, s: (0, 0)),
                pl.BlockSpec((t, m), lambda j, s: (0, 0)),
                pl.BlockSpec((t, width), lambda j, s: (0, s[0, j])),
                pl.BlockSpec((t, width), lambda j, s: (0, s[0, j])),
            ],
            out_specs=[
                pl.BlockSpec((1, m, width), lambda j, s: (jnp.minimum(j, half - 1), 0, 0)),
                pl.BlockSpec((1, m, width), lambda j, s: (jnp.maximum(j - half, 0), 0, 0)),
            ],
        ),
        cost_estimate=cost(4 * t * m * pieces * width, 2 * (2 * t * m + 2 * t * width * pieces + m * pieces * width)),
    )(plan.grad_idx, ao, ap, bo, bp)


def finish_kernel(count, idx, *refs):
    out = refs[-1]
    for k in range(count):

        @pl.when(pl.program_id(0) == k)
        def _():
            out[...] = refs[k][...].astype(F32).reshape(out.shape)


def finish(plan, own, partner, total, shape, where):
    pieces = list(own) + list(partner)
    block, index = where
    count = len(pieces)
    in_specs = [pl.BlockSpec(p.shape, lambda i, s: (0, 0)) for p in pieces]
    args = [plan.place_idx] + pieces
    alias = {}
    if total is not None:
        in_specs.append(pl.BlockSpec(memory_space=pl.ANY))
        alias = {len(args): 0}
        args.append(total)
    return pl.pallas_call(
        functools.partial(finish_kernel, count), name="finish",
        out_shape=jax.ShapeDtypeStruct(shape, F32),
        grid_spec=pltpu.PrefetchScalarGridSpec(
            num_scalar_prefetch=1, grid=(count,), in_specs=in_specs,
            out_specs=pl.BlockSpec(block, lambda i, s: index(s[i])),
        ),
        input_output_aliases=alias,
        cost_estimate=cost(0, 6 * count * pieces[0].size),
    )(*args)


class Plan:
    def __init__(self, size):
        bits = size.bit_length() - 1
        assert size == 1 << bits and bits >= 2, size
        self.size, self.stages = size, bits - 1
        self.pieces = 1 << self.stages
        upper = list(range(1, bits))
        self.orders = [upper, upper[1:] + upper[:1]]
        self.swap = [(i, i ^ 1) for i in range(size)]
        self.perms = [
            [(i, i ^ (1 << self.orders[i & 1][s])) for i in range(size)] for s in range(self.stages)
        ]
        me = lax.axis_index("replica")
        core = me & 1

        def place(c, j):
            out = 0
            for s in range(self.stages):
                bit = self.orders[c][s]
                js = (j >> (self.stages - 1 - s)) & 1
                out = out + (((me >> bit) & 1) ^ js) * (1 << (bit - 1))
            return out

        half = self.pieces // 2
        mine = [jnp.where(core == 0, place(0, j), place(1, j)) for j in range(self.pieces)]
        theirs = [jnp.where(core == 0, place(1, j), place(0, j)) for j in range(self.pieces)]
        turned = [mine[(j + half) % self.pieces] for j in range(self.pieces)]
        whole = [core * self.pieces + v for v in turned]
        self.grad_idx = jnp.stack([jnp.stack(whole), jnp.stack(turned)]).astype(jnp.int32)
        self.place_idx = jnp.stack(
            [core * self.pieces + v for v in mine] + [(1 - core) * self.pieces + v for v in theirs]
        ).astype(jnp.int32)
        self.core = core

    def pair(self, x):
        return lax.ppermute(x, "replica", self.swap)

    def stage(self, x, s):
        return lax.ppermute(x, "replica", self.perms[s])


def other_half(plan, x):
    n = x.shape[1] // 2
    return lax.dynamic_slice_in_dim(x, (1 - plan.core) * n, n, axis=1)


def reduce_chunk(plan, send, keep, label):
    for s in range(plan.stages):
        with jax.named_scope(f"rs{s}_{label}"):
            got = plan.stage(send, s)
        n = got.shape[0]
        added = lambda part: (keep[part].astype(F32) + got[part].astype(F32)).astype(BF16)
        if n == 1:
            held = {0: added(0)}
        else:
            send, keep = added(slice(n // 2, n)), added(slice(0, n // 2))
    for s in reversed(range(plan.stages)):
        bit = 1 << (plan.stages - 1 - s)
        with jax.named_scope(f"ag{s}_{label}"):
            for j in list(held):
                held[j | bit] = plan.stage(held[j], s)
    with jax.named_scope(f"swap_{label}"):
        partner = {j: plan.pair(v) for j, v in held.items()}
    return [held[j] for j in range(plan.pieces)], [partner[j] for j in range(plan.pieces)]


def butterfly(plan, x):
    for b in range(plan.stages + 1):
        perm = [(i, i ^ (1 << b)) for i in range(plan.size)]
        x = x + lax.ppermute(x, "replica", perm)
    return x


def scatter_shard(x, size, axis):
    me = lax.axis_index("shard")
    n = x.shape[axis] // size
    block = lambda k: lax.dynamic_slice_in_dim(x, ((me + k) % size) * n, n, axis=axis)
    total = block(0).astype(F32)
    for k in range(1, size):
        perm = [(i, (i + k) % size) for i in range(size)]
        total = total + lax.ppermute(block(k), "shard", perm).astype(F32)
    return total


def shards(sizes, inputs, lengths, ln_gain, ln_bias, qkv_weight, qkv_bias, out_weight,
           fc1_weight, fc1_bias, fc2_weight, out_bias, cotangent):
    replicas, zs = sizes
    plan = Plan(replicas)
    w3 = jnp.transpose(qkv_weight, (1, 0, 2))
    normed = norm(inputs, ln_gain, ln_bias)
    normed = lax.all_gather(normed, "shard", axis=0, tiled=True)
    cot = lax.all_gather(cotangent, "shard", axis=0, tiled=True)
    count, width = normed.shape
    tab, bias = tables(lengths[0], count)

    hidden, slope = fc1(normed, fc1_weight, fc1_bias)
    by_rows = hidden.shape[1] % (2 * plan.pieces * LANES) == 0
    hidden_p = plan.pair(other_half(plan, hidden) if by_rows else hidden)
    normed_p = plan.pair(other_half(plan, normed))
    qkv = project(normed, w3, qkv_bias, tab)
    cot_p = plan.pair(cot)
    grad_ctx = lax.dot_general(cot, out_weight, NT, preferred_element_type=F32).astype(BF16)

    results = {}

    def run(name, shape, chunks, where):
        total = None
        for label, pieces, spot in chunks:
            own, partner = reduce_chunk(plan, *pieces, f"{name}{label}")
            total = finish(plan, own, partner, total, shape, where(spot))
        results[name] = total

    context, grad_qkv, grad_qkv_b = attention(qkv, grad_ctx, tab, bias)
    context_p = plan.pair(context)
    grad_pre, grad_fc1_b = gradpre(cot, fc2_weight, slope)
    grad_pre_p = plan.pair(grad_pre)
    grad_qkv_p = plan.pair(grad_qkv)

    hid = hidden.shape[1]
    rows2 = hid // (2 * plan.pieces)

    def cut(n, widths):
        out, at = [], 0
        for w in widths:
            out.append((at, w))
            at += w
        assert at == n
        return out

    n_ctx = context.shape[1]
    cols = width // (2 * plan.pieces)
    if by_rows:
        run("fc2", (hid, width), [
            (k, grad_rows(plan, hidden, hidden_p, cot, cot_p, at, w), (at, w))
            for k, (at, w) in enumerate(cut(width, [width // 4, width // 4, width // 2]))
        ], lambda s: ((rows2, s[1]), lambda r: (r, s[0] // s[1])))
    else:
        run("fc2", (hid, width), [(0, grad_cols(plan, hidden, hidden_p, cot, cot_p), None)],
            lambda s: ((hid, cols), lambda r: (0, r)))
    run("out", (n_ctx, width), [(0, grad_cols(plan, context, context_p, cot, cot_p), None)],
        lambda s: ((n_ctx, cols), lambda r: (0, r)))
    rows1 = width // (2 * plan.pieces)
    run("fc1", (width, hid), [
        (k, grad_rows(plan, normed, normed_p, grad_pre, grad_pre_p, at, w), (at, w))
        for k, (at, w) in enumerate(cut(hid, [hid // 2, hid // 2]))
    ], lambda s: ((rows1, s[1]), lambda r: (r, s[0] // s[1])))
    run("qkv", (3, width, n_ctx), [
        (k, grad_rows(plan, normed, normed_p, grad_qkv[k], grad_qkv_p[k], 0, n_ctx), k)
        for k in (2, 1, 0)
    ], lambda s: ((1, rows1, n_ctx), lambda r: (s, r, 0)))

    mixed = (
        jnp.dot(context, out_weight, preferred_element_type=F32)
        + jnp.dot(hidden, fc2_weight, preferred_element_type=F32)
    ).astype(BF16)
    x_float = inputs.astype(F32)
    output = (x_float + scatter_shard(mixed, zs, 0) + out_bias).astype(BF16)

    back = lax.dot_general(grad_pre, fc1_weight, NT, preferred_element_type=F32)
    for k in range(3):
        back = back + lax.dot_general(grad_qkv[k], w3[k], NT, preferred_element_type=F32)
    grad_normed = scatter_shard(back.astype(BF16), zs, 0)

    mean = jnp.mean(x_float, axis=-1, keepdims=True)
    cen = x_float - mean
    inv_std = lax.rsqrt(jnp.mean(cen * cen, axis=-1, keepdims=True) + 1e-05)
    x_hat = cen * inv_std
    parts = jnp.stack([jnp.sum(grad_normed * x_hat, axis=0), jnp.sum(grad_normed, axis=0)])
    scaled = grad_normed * ln_gain
    input_grad = cotangent.astype(F32) + inv_std * (
        scaled
        - jnp.mean(scaled, axis=-1, keepdims=True)
        - x_hat * jnp.mean(scaled * x_hat, axis=-1, keepdims=True)
    )
    share = scatter_shard(parts, zs, 1)
    out_b = jnp.sum(cot, axis=0, dtype=F32)
    small = jnp.concatenate(
        [share.reshape(-1), grad_qkv_b.reshape(-1), grad_fc1_b.reshape(-1), out_b]
    )
    small = butterfly(plan, small.reshape(-1, LANES)).reshape(-1)
    n_ln = share.shape[1]
    ends = [n_ln, 2 * n_ln, 2 * n_ln + 3 * n_ctx, 2 * n_ln + 3 * n_ctx + hid]
    gain_g, bias_g, qkv_b, fc1_b, out_bg = jnp.split(small, ends)
    return (
        output, input_grad, gain_g, bias_g,
        jnp.transpose(results["qkv"], (1, 0, 2)), qkv_b.reshape(3, n_ctx),
        results["out"], results["fc1"], fc1_b, results["fc2"], out_bg,
    )


def solution(mesh):
    rows, row, col = P(("replica", "shard"), None), P("shard", None), P(None, "shard")
    return jax.shard_map(
        functools.partial(shards, (mesh.shape["replica"], mesh.shape["shard"])),
        mesh=mesh,
        in_specs=(
            rows, P("replica", None), P(), P(), P(None, None, "shard"), col, row, col, P("shard"),
            row, P(), rows,
        ),
        out_specs=(
            rows, rows, P("shard"), P("shard"), P(None, None, "shard"), col, row, col, P("shard"),
            row, P(),
        ),
        check_vma=False,
    )
```
